32 devices in a mesh: width: 4 (over z), row: 4 (over y, core), src: 2 (over x).
Axes of the slice: x: 2, y: 2, z: 4, core: 2. Of those that a mesh axis runs over, the one named last changes fastest.
Arguments:
- query_rows: bfloat16 [1024, 8192], P('row', 'width'), may hold values from -150 to 150
- key_rows: bfloat16 [1024, 1024], P('src', 'width'), may hold values from -7 to 7
- value_rows: bfloat16 [1024, 1024], P('src'), may hold values from -6 to 6
- out_proj: bfloat16 [8192, 8192], P(('row', 'src'), 'width'), may hold values from -0.0625 to 0.0625
Outputs:
- share: float32 [1024, 1024], P('row', ('src', 'width'))
The draws below stay inside these ranges and needn't reach their ends.
All inputs are finite; a program needn't handle non-finite values.
Results may differ from the reference program's by a relative error of at most 0.0014.
Values may be sent and summed in bfloat16 or wider, within the bound.
No kernel may reach another device: no remote copies, remote signals or barrier semaphores. Data moves between devices by JAX's collectives and lax.ppermute only.
A program may use at most 384 MiB of HBM per device.

```python
import jax
import jax.numpy as jnp
from jax import lax

D = 8192
H = 64
KV = 8
HD = 128
SEQ = 1024


def final_keys(key):
    normal_keys = jnp.clip(jax.random.normal(jax.random.fold_in(key, 11), (SEQ, KV * HD), jnp.float32), -6.0, 6.0)
    return normal_keys


def draw_key_rows(key, part):
    return final_keys(key).astype(jnp.bfloat16)


def draw_query_rows(key, part):
    result = jnp.clip(jax.random.normal(jax.random.fold_in(key, 21), (SEQ, H * HD), jnp.float32), -6.0, 6.0)
    return result.astype(jnp.bfloat16)


def block_scale(own_key, shape, shards, smallest, high):
    gain = 1.0
    for axis_at, shards_of in shards:
        draws = jax.random.uniform(jax.random.fold_in(jax.random.fold_in(own_key, 6), axis_at), (shards_of,), jnp.float32, smallest / len(shards), high / len(shards))
        gain = gain * jnp.repeat(jnp.exp(draws), shape[axis_at] // shards_of).reshape((-1,) + (1,) * (len(shape) - 1 - axis_at))
    return gain


def bell_draw(key, dims, spread, reach, cuts=(), kind=jnp.bfloat16):
    level = block_scale(key, dims, cuts, -0.22, 0.18) if cuts else 1.0
    array = jax.random.normal(key, dims, jnp.float32) * spread * level
    return jnp.minimum(jnp.maximum(array, -reach), reach).astype(kind)


def setup_inputs(seed: int = 0) -> dict:
    key_of = jax.random.split(jax.random.key(seed), 5)
    return {
        "query_rows": draw_query_rows(jax.random.fold_in(key_of[4], 71), 0),
        "key_rows": draw_key_rows(jax.random.fold_in(key_of[4], 71), 0),
        "value_rows": bell_draw(key_of[2], (SEQ, KV * HD), 1.0, 6.0, ((0, 2),)),
        "out_proj": bell_draw(key_of[3], (H * HD, D), (H * HD) ** -0.5, 0.0625, ((0, 8), (1, 4))),
    }


def reference(query_rows, key_rows, value_rows, out_proj):
    group_size = H // KV
    queries = query_rows.astype(jnp.float32).reshape(SEQ, KV, group_size, HD)
    key_heads = key_rows.astype(jnp.float32).reshape(SEQ, KV, HD)
    scores = jnp.einsum('ikgd,jkd->kgij', queries, key_heads).reshape(H, SEQ, SEQ) / jnp.sqrt(jnp.float32(HD))
    positions = jnp.arange(SEQ, dtype=jnp.int32)
    causal = positions[:, None] >= positions[None, :]
    masked = jnp.where(causal, scores, jnp.float32(-1e+30))
    row_peak = lax.optimization_barrier(jnp.max(masked, axis=-1, keepdims=True))
    shifted = jnp.where(causal, jnp.exp(masked - row_peak), jnp.float32(0.0))
    weights = (shifted / lax.optimization_barrier(jnp.sum(shifted, axis=-1, keepdims=True))).astype(jnp.bfloat16)
    value_heads = value_rows.astype(jnp.float32).reshape(SEQ, KV, HD)
    proj_heads = out_proj.astype(jnp.float32).reshape(KV, group_size, HD, D)

    def image_one(kv_index):
        value_kv = jnp.take(value_heads, kv_index, axis=1)
        weight_kv = jnp.take(proj_heads, kv_index, axis=0)
        return jnp.einsum('jd,gde->jge', value_kv, weight_kv).astype(jnp.bfloat16)
    images = lax.map(image_one, jnp.arange(KV, dtype=jnp.int32))
    images = images.transpose(1, 0, 2, 3).reshape(SEQ, H, D)
    blocks = SEQ // 8
    weight_blocks = weights.reshape(H, SEQ, blocks, 8).transpose(2, 0, 1, 3)
    image_blocks = images.reshape(blocks, 8, H, D)

    def norm_block(operands):
        attend, source_images = operands
        contrib = jnp.einsum('hij,jhe->jie', attend.astype(jnp.float32), source_images.astype(jnp.float32))
        return lax.optimization_barrier(jnp.sum(jnp.abs(contrib), axis=-1))
    norms_table = lax.map(norm_block, (weight_blocks, image_blocks)).reshape(SEQ, SEQ).T
    totals = lax.optimization_barrier(jnp.sum(norms_table, axis=1, keepdims=True))
    return (positions + 1).astype(jnp.float32)[:, None] * norms_table / totals
```

```python
import functools
import math

import jax
import jax.numpy as jnp
from jax import lax
from jax.experimental import pallas as pl
from jax.experimental.pallas import tpu as pltpu
from jax.sharding import PartitionSpec as P

H = 64
KV = 8
HD = 128
GROUP = H // KV
LANES = 128
CHUNKS = 2


def rotated(value, axis, shift):
    size = lax.axis_size(axis)
    return lax.ppermute(value, axis, [(k, (k + shift) % size) for k in range(size)])


def gathered(value, axis):
    size = lax.axis_size(axis)
    return [value] + [rotated(value, axis, shift) for shift in range(1, size)]


def in_order(entries, axis):
    size = len(entries)
    here = lax.axis_index(axis)
    stacked = jnp.stack(entries[::-1])
    return jnp.roll(stacked, here + 1, axis=0) if size > 1 else stacked


def exchanged(blocks, axis):
    size = lax.axis_size(axis)
    here = lax.axis_index(axis)
    result = []
    for bit in range(size):
        block = lax.dynamic_index_in_dim(blocks, here ^ bit, 0, keepdims=False)
        if bit:
            block = lax.ppermute(block, axis, [(k, k ^ bit) for k in range(size)])
        result.append(block)
    return result


def weights_kernel(place_ref, q_ref, k_ref, o_ref, stage, *, rows, parts, here_heads, limits, scale):
    here_src = place_ref[0]
    half = rows // parts // 2
    piece = rows // parts
    for block, (low, high) in enumerate(limits):

        @pl.when(pl.program_id(0) == block)
        def _(block=block, low=low, high=high):
            local = block * LANES + lax.broadcasted_iota(jnp.int32, (1, LANES), 1)
            inner = local % piece
            sub = jnp.where(inner < half, here_src, 2 * parts - 1 - here_src)
            position = local // piece * rows + sub * half + inner % half
            source = low + lax.broadcasted_iota(jnp.int32, (high - low, LANES), 0)
            causal = source <= position
            for group in range(here_heads // GROUP):
                keys = k_ref[0:high, group * HD : (group + 1) * HD]

                def head(step, carry, group=group, keys=keys):
                    at = group * GROUP + step
                    query = q_ref[:, pl.ds(pl.multiple_of(at * HD, HD), HD)]
                    scores = lax.dot_general(
                        keys, query, (((1,), (1,)), ((), ())), preferred_element_type=jnp.float32
                    )
                    edge = jnp.where(causal, scores[low:high], jnp.float32(-1e30))
                    scores = jnp.concatenate([scores[:low], edge], axis=0) if low else edge
                    peak = jnp.max(scores, axis=0, keepdims=True)
                    grown = jnp.exp2((scores - peak) * scale)
                    mass = jnp.sum(grown, axis=0, keepdims=True)
                    stage[pl.ds(at, high, stride=here_heads), :] = grown * (1.0 / mass)
                    return carry

                lax.fori_loop(0, GROUP, head, 0)

            chunk = 32

            def cast(step, carry):
                start = pl.multiple_of(step * chunk * here_heads, chunk * here_heads)
                value = stage[pl.ds(start, chunk * here_heads), :]
                o_ref[pl.ds(pl.multiple_of(step * chunk, chunk), chunk)] = value.reshape(
                    chunk, here_heads, LANES
                ).astype(jnp.bfloat16)
                return carry

            lax.fori_loop(0, high // chunk, cast, 0)


def head_weights(place, queries, keys, rows, parts):
    count, width = queries.shape
    sources = keys.shape[0]
    here_heads = width // HD
    piece = rows // parts
    blocks = count // LANES
    limits = []
    for block in range(blocks):
        low = block * LANES // piece * rows
        high = (((block + 1) * LANES - 1) // piece + 1) * rows
        limits.append((low, high))
    kernel = functools.partial(
        weights_kernel,
        rows=rows,
        parts=parts,
        here_heads=here_heads,
        limits=limits,
        scale=math.log2(math.e) / math.sqrt(HD),
    )
    work = count * sources * here_heads
    return pl.pallas_call(
        kernel,
        out_shape=jax.ShapeDtypeStruct((sources, here_heads, count), jnp.bfloat16),
        grid_spec=pltpu.PrefetchScalarGridSpec(
            num_scalar_prefetch=1,
            grid=(blocks,),
            in_specs=[
                pl.BlockSpec((LANES, width), lambda b, place: (b, 0)),
                pl.BlockSpec(keys.shape, lambda b, place: (0, 0)),
            ],
            out_specs=pl.BlockSpec((sources, here_heads, LANES), lambda b, place: (0, 0, b)),
            scratch_shapes=[pltpu.VMEM((sources * here_heads, LANES), jnp.float32)],
        ),
        compiler_params=pltpu.CompilerParams(vmem_limit_bytes=60 << 20),
        cost_estimate=pl.CostEstimate(
            flops=work * HD, transcendentals=work // 2, bytes_accessed=work * 2
        ),
        name="head_weights",
    )(place, queries, keys)


def norms_kernel(place_ref, v_ref, *refs, rows, parts, spans, first, sub_cols):
    here_src = place_ref[0]
    count = refs[0].shape[-1]
    wo_refs = refs[: parts]
    w_refs = refs[parts : parts + spans]
    rest = refs[parts + spans :]
    if first:
        o_ref, stage = rest
        o_ref[...] = jnp.zeros_like(o_ref)
    else:
        before_ref, o_ref, stage = rest
        o_ref[...] = before_ref[...]
    sources = v_ref.shape[0]
    row_devices, local_rows, cols = wo_refs[0].shape
    local_heads = local_rows // HD
    piece = rows // parts
    half = piece // 2
    total = w_refs[0].shape[-1]
    subs = total // half
    for turn in range(parts):
        origin = lax.rem(here_src + parts - turn, parts)
        for row in range(row_devices):
            base = (row * parts + origin) * local_heads

            def image(step, carry, turn=turn, row=row, base=base):
                head = base + step
                group = head // GROUP
                values = v_ref[:, pl.ds(pl.multiple_of(group * HD, HD), HD)]
                part = wo_refs[turn][row, pl.ds(pl.multiple_of(step * HD, HD), HD), :]
                made = jnp.dot(values, part, preferred_element_type=jnp.float32)
                for col in range(cols // LANES):
                    stage[col, pl.ds(head, sources, stride=H), :] = made[
                        :, col * LANES : (col + 1) * LANES
                    ]
                return carry

            lax.fori_loop(0, local_heads, image, 0)

    col_base = pl.program_id(0) * sources
    lane = lax.broadcasted_iota(jnp.int32, (total, LANES), 1)
    for block in range(sources // sub_cols):
        start_col = col_base + block * sub_cols
        skip = jnp.int32(0)
        for sub in range(subs):
            row, side = sub // 2, sub % 2
            at = here_src if side == 0 else 2 * parts - 1 - here_src
            last = row * rows + (at + 1) * half - 1
            skip = skip + jnp.where(last < start_col, 1, 0).astype(jnp.int32)
        for sub in range(subs):

            @pl.when(skip == sub)
            def _(sub=sub, block=block):
                begin = sub * half
                aligned = begin // LANES * LANES

                def one(step, acc):
                    for inner in range(2):
                        col = block * sub_cols + step * 2 + inner
                        attend = jnp.concatenate(
                            [ref[col, :, aligned:] for ref in w_refs], axis=0
                        )
                        made = jnp.concatenate(
                            [
                                stage[k, pl.ds(pl.multiple_of(col * H, H), H), :].astype(
                                    jnp.bfloat16
                                )
                                for k in range(cols // LANES)
                            ],
                            axis=1,
                        )
                        contrib = jnp.dot(
                            attend.T[begin - aligned :], made, preferred_element_type=jnp.float32
                        )
                        norm = jnp.sum(jnp.abs(contrib), axis=1, keepdims=True)
                        acc = jnp.where(lane[begin:] == col, norm, acc)
                    return acc

                found = lax.fori_loop(
                    0, sub_cols // 2, one, jnp.zeros((total - begin, LANES), jnp.float32)
                )
                o_ref[begin:, :] += found


def partial_norms(place, values, projections, weights, before, rows, parts):
    sources = values.shape[0]
    count = weights[0].shape[-1]
    cols = projections[0].shape[-1]
    step = LANES
    grid = sources // step
    half = rows // parts // 2
    kernel = functools.partial(
        norms_kernel,
        rows=rows,
        parts=parts,
        spans=len(weights),
        first=before is None,
        sub_cols=min(64, step),
    )
    in_specs = [pl.BlockSpec((step, values.shape[1]), lambda b, place: (b, 0))]
    in_specs += [
        pl.BlockSpec(p.shape, lambda b, place: (0, 0, 0), pipeline_mode=pl.Buffered(1))
        for p in projections
    ]
    in_specs += [
        pl.BlockSpec((step,) + w.shape[1:], lambda b, place: (b, 0, 0)) for w in weights
    ]
    args = [values, *projections, *weights]
    out_spec = pl.BlockSpec((count, step), lambda b, place: (0, b))
    if before is not None:
        in_specs.append(out_spec)
        args.append(before)
    return pl.pallas_call(
        kernel,
        out_shape=jax.ShapeDtypeStruct((count, sources), jnp.float32),
        grid_spec=pltpu.PrefetchScalarGridSpec(
            num_scalar_prefetch=1,
            grid=(grid,),
            in_specs=in_specs,
            out_specs=out_spec,
            scratch_shapes=[pltpu.VMEM((cols // LANES, step * H, LANES), jnp.float32)]
            if cols >= LANES
            else [pltpu.VMEM((1, step * H, cols), jnp.float32)],
        ),
        compiler_params=pltpu.CompilerParams(vmem_limit_bytes=60 << 20),
        cost_estimate=pl.CostEstimate(
            flops=count * sources * H * cols + 2 * sources * H * HD * cols,
            transcendentals=0,
            bytes_accessed=count * sources * H * 2,
        ),
        name="partial_norms",
    )(place, *args)


def body(query_rows, key_rows, value_rows, out_proj):
    row_devices = lax.axis_size("row")
    parts = lax.axis_size("src")
    spans = lax.axis_size("width")
    here_row = lax.axis_index("row")
    here_src = lax.axis_index("src")
    rows, width = query_rows.shape
    piece = rows // parts
    half = piece // 2
    place = here_src.astype(jnp.int32).reshape(1)

    subs = query_rows.reshape(2 * parts, half, width)
    mine = jnp.concatenate(
        [
            lax.dynamic_index_in_dim(subs, here_src, 0, keepdims=False),
            lax.dynamic_index_in_dim(subs, 2 * parts - 1 - here_src, 0, keepdims=False),
        ],
        axis=0,
    )
    queries = lax.all_gather(mine, "row", axis=0, tiled=True)
    keys = in_order(gathered(key_rows, "src"), "src").reshape(-1, key_rows.shape[1])
    values = in_order(gathered(value_rows, "src"), "src").reshape(-1, value_rows.shape[1])
    query_list = lax.all_gather(queries, "width", axis=0)
    key_list = lax.all_gather(keys, "width", axis=0)
    weights = [
        head_weights(place, query_list[k], key_list[k], rows, parts) for k in range(spans)
    ]

    local_rows, cols = out_proj.shape
    each = cols // row_devices
    chunks = CHUNKS if each % (CHUNKS * LANES) == 0 else 1
    split = out_proj.reshape(local_rows, row_devices, chunks, each // chunks)
    norms = None
    for chunk in range(chunks):
        blocks = split[:, :, chunk].transpose(1, 0, 2)
        moved = lax.all_to_all(blocks, "row", split_axis=0, concat_axis=0, tiled=True)
        projections = gathered(moved, "src")
        norms = partial_norms(place, values, projections, weights, norms, rows, parts)

    mine = lax.psum_scatter(norms, "row", scatter_dimension=0, tiled=True)
    sources = mine.shape[1]
    halves = mine.reshape(piece, parts, sources // parts).transpose(1, 0, 2)
    halves = lax.all_to_all(halves, "src", split_axis=0, concat_axis=0, tiled=True)
    halves = halves.reshape(parts, 2, half, -1)
    table = jnp.concatenate([halves[:, 0], halves[::-1, 1]], axis=0).reshape(rows, -1)
    summed = lax.psum_scatter(table, "width", scatter_dimension=1, tiled=True)
    totals = lax.psum(jnp.sum(summed, axis=1), ("width", "src"))
    position = (here_row * rows + jnp.arange(rows, dtype=jnp.int32) + 1).astype(jnp.float32)
    return position[:, None] * summed / totals[:, None]


def solution(mesh):
    placed = (P("row", "width"), P("src", "width"), P("src", None), P(("row", "src"), "width"))
    return jax.shard_map(
        body, mesh=mesh, in_specs=placed, out_specs=P("row", ("src", "width")), check_vma=False
    )
```

```python
import functools
import math

import jax
import jax.numpy as jnp
from jax import lax
from jax.experimental import pallas as pl
from jax.experimental.pallas import tpu as pltpu
from jax.sharding import PartitionSpec as P

H = 64
KV = 8
HD = 128
GROUP = H // KV
LANES = 128
CHUNKS = 2


def rotated(value, axis, shift):
    size = lax.axis_size(axis)
    return lax.ppermute(value, axis, [(k, (k + shift) % size) for k in range(size)])


def gathered(value, axis):
    size = lax.axis_size(axis)
    return [value] + [rotated(value, axis, shift) for shift in range(1, size)]


def in_order(entries, axis):
    size = len(entries)
    here = lax.axis_index(axis)
    stacked = jnp.stack(entries[::-1])
    return jnp.roll(stacked, here + 1, axis=0) if size > 1 else stacked


def swapped(value, axis, bit):
    size = lax.axis_size(axis)
    return lax.ppermute(value, axis, [(k, k ^ bit) for k in range(size)])


def spread(value, axis):
    size = lax.axis_size(axis)
    held = {0: value}
    bit = size // 2
    while bit:
        held.update({k | bit: swapped(v, axis, bit) for k, v in list(held.items())})
        bit //= 2
    return [held[k] for k in range(size)]


def shared_halves(value):
    count = value.shape[0]
    odd = lax.axis_index("row") % 2
    half = lax.dynamic_slice_in_dim(value, odd * (count // 2), count // 2, 0)
    mine = in_order(gathered(half, "src"), "src")
    other = swapped(mine, "row", 1)
    first = jnp.where(odd == 0, mine, other)
    second = jnp.where(odd == 0, other, mine)
    return jnp.stack([first, second], axis=1).reshape((-1,) + value.shape[1:])


def line_gather(value, axis):
    size = lax.axis_size(axis)
    here = lax.axis_index(axis)
    up, down = [value], [value]
    for _ in range(size - 1):
        up.append(lax.ppermute(up[-1], axis, [(k, k + 1) for k in range(size - 1)]))
        down.append(lax.ppermute(down[-1], axis, [(k + 1, k) for k in range(size - 1)]))
    order = [
        sorted((k for k in range(size) if k != at), key=lambda k: abs(k - at)) for at in range(size)
    ]
    values, origins = [value], [here]
    for slot in range(size - 1):
        origin = jnp.array([order[at][slot] for at in range(size)], jnp.int32)[here]
        picked = None
        for at in range(size):
            far = order[at][slot] - at
            entry = down[far] if far > 0 else up[-far]
            picked = entry if picked is None else jnp.where(here == at, entry, picked)
        values.append(picked)
        origins.append(origin)
    return values, origins


PAD = 8
UNROLL = 32
HEADS_TOGETHER = 4
STEP = 128


def piece_starts(here_src, rows, parts, row_devices):
    piece = rows // parts
    return [
        row * rows + (here_src if row % 2 == 0 else parts - 1 - here_src) * piece
        for row in range(row_devices)
    ]


def weights_kernel(
    place_ref, *refs, rows, parts, row_devices, sources, limits, scale
):
    pieces = refs[:row_devices]
    o_ref, stage, scales, held, keys = refs[row_devices:]
    here_src, here_row = place_ref[0], place_ref[1]
    piece = rows // parts
    here_heads = held.shape[1] // HD
    key_width = keys.shape[1]
    chunk = math.gcd(rows, 256)
    packs = held.shape[1] // key_width
    pack_rows = pieces[0].shape[0] - piece
    share = sources // parts // row_devices
    step_at = pl.program_id(0)

    @pl.when(step_at == 0)
    def _():
        for bit, ref in enumerate(pieces):
            origin = here_row ^ bit
            for pack in range(packs):
                src, inner = divmod(pack * pack_rows, share)
                at = src * (sources // parts) + origin * share + inner
                keys[pl.ds(pl.multiple_of(at, pack_rows), pack_rows), :] = ref[
                    piece:, pack * key_width : (pack + 1) * key_width
                ]

    per = max(1, LANES // piece)
    for slot in range(per):
        want = step_at * per + slot
        for bit, ref in enumerate(pieces):

            @pl.when(here_row ^ bit == want)
            def _(ref=ref, slot=slot):
                held[slot * piece : (slot + 1) * piece, :] = ref[:piece, :]

    def folded(value, combine):
        return combine(value.reshape(-1, 8, LANES), axis=0)

    for block, (low, high) in enumerate(limits):

        @pl.when(step_at == block)
        def _(block=block, low=low, high=high):
            local = block * LANES + lax.broadcasted_iota(jnp.int32, (1, LANES), 1)
            row = local // piece
            turn = jnp.where(row % 2 == 0, here_src, parts - 1 - here_src)
            position = row * rows + turn * piece + local % piece
            together = math.gcd(HEADS_TOGETHER, here_heads)

            def several(step, carry):
                for inner in range(together):
                    head = step * together + inner
                    group = head // GROUP
                    query = held[:, pl.ds(pl.multiple_of(head * HD, HD), HD)]
                    columns = pl.ds(pl.multiple_of(group * HD, HD), HD)
                    peak = jnp.full((8, LANES), -1e30, jnp.float32)
                    for at in range(0, high, chunk):
                        scores = lax.dot_general(
                            keys[at : at + chunk, columns],
                            query,
                            (((1,), (1,)), ((), ())),
                            preferred_element_type=jnp.float32,
                        )
                        if at >= low:
                            source = at + lax.broadcasted_iota(jnp.int32, (chunk, LANES), 0)
                            scores = jnp.where(source <= position, scores, jnp.float32(-1e30))
                        stage[head, at : at + chunk, :] = scores
                        peak = jnp.maximum(peak, folded(scores, jnp.max))
                    peak = jnp.max(peak, axis=0, keepdims=True)
                    mass = jnp.zeros((8, LANES), jnp.float32)
                    for at in range(0, high, chunk):
                        grown = jnp.exp2((stage[head, at : at + chunk, :] - peak) * scale)
                        stage[head, at : at + chunk, :] = grown
                        mass = mass + folded(grown, jnp.sum)
                    mass = jnp.sum(mass, axis=0, keepdims=True)
                    scales[pl.ds(pl.multiple_of(head * 8, 8), 8), :] = jnp.broadcast_to(
                        1.0 / mass, (8, LANES)
                    )
                return carry

            lax.fori_loop(0, here_heads // together, several, 0)
            flat = stage.reshape(here_heads * (sources + PAD), LANES)
            factors = scales[pl.ds(0, here_heads, stride=8), :]
            each = 16

            def cast(step, carry):
                for inner in range(each):
                    at = step * each + inner
                    value = flat[pl.ds(at, here_heads, stride=sources + PAD), :]
                    o_ref[at] = (value * factors).astype(jnp.bfloat16)
                return carry

            lax.fori_loop(0, high // each, cast, 0, unroll=2)


def head_weights(place, pieces, rows, parts, sources, key_width):
    height, width = pieces[0].shape
    row_devices = len(pieces)
    here_heads = width // HD
    piece = rows // parts
    count = piece * row_devices
    blocks = count // LANES
    limits = [
        (
            block * LANES // piece * rows,
            (((block + 1) * LANES - 1) // piece + 1) * rows,
        )
        for block in range(blocks)
    ]
    kernel = functools.partial(
        weights_kernel,
        rows=rows,
        parts=parts,
        row_devices=row_devices,
        sources=sources,
        limits=limits,
        scale=math.log2(math.e) / math.sqrt(HD),
    )
    work = count * sources * here_heads
    return pl.pallas_call(
        kernel,
        out_shape=jax.ShapeDtypeStruct((blocks, sources, here_heads, LANES), jnp.bfloat16),
        grid_spec=pltpu.PrefetchScalarGridSpec(
            num_scalar_prefetch=1,
            grid=(blocks,),
            in_specs=[
                pl.BlockSpec((height, width), lambda b, place: (0, 0), pipeline_mode=pl.Buffered(1))
            ]
            * row_devices,
            out_specs=pl.BlockSpec(
                (None, sources, here_heads, LANES), lambda b, place: (b, 0, 0, 0)
            ),
            scratch_shapes=[
                pltpu.VMEM((here_heads, sources + PAD, LANES), jnp.float32),
                pltpu.VMEM((here_heads * 8, LANES), jnp.float32),
                pltpu.VMEM((LANES, width), jnp.bfloat16),
                pltpu.VMEM((sources, key_width), jnp.bfloat16),
            ],
        ),
        compiler_params=pltpu.CompilerParams(vmem_limit_bytes=60 << 20),
        cost_estimate=pl.CostEstimate(
            flops=work * HD, transcendentals=work // 2, bytes_accessed=work * 2
        ),
        name="head_weights",
    )(place, *pieces)


def norms_kernel(place_ref, v_ref, *refs, rows, parts, row_devices, spans, first):
    here_src, here_row = place_ref[0], place_ref[1]
    wo_refs = refs[: parts * row_devices]
    w_refs = refs[parts * row_devices : parts * row_devices + spans]
    rest = refs[parts * row_devices + spans :]
    if first:
        o_ref, stage, flipped = rest
    else:
        before_ref, o_ref, stage, flipped = rest
    sources = v_ref.shape[0]
    local_rows, cols = wo_refs[0].shape
    span_heads = H // spans
    local_heads = local_rows // HD
    piece = rows // parts
    pitch = sources + PAD
    tiles = range(cols // LANES)
    blocks = w_refs[0].shape[0]
    for turn in range(parts):
        origin = lax.rem(here_src + parts - turn, parts)
        for bit in range(row_devices):
            base = ((here_row ^ bit) * parts + origin) * local_heads
            for step in range(local_heads):
                head = base + step
                group = head // GROUP
                values = v_ref[:, pl.ds(pl.multiple_of(group * HD, HD), HD)]
                part = wo_refs[bit * parts + turn][step * HD : (step + 1) * HD, :]
                made = jnp.dot(values, part, preferred_element_type=jnp.float32)
                at = pl.multiple_of(head * pitch, PAD)
                for tile in tiles:
                    stage[tile, pl.ds(at, sources), :] = made[:, tile * LANES : (tile + 1) * LANES]

    slots = [place_ref[2 + k] * (span_heads * pitch) for k in range(spans)]
    start = pl.program_id(0) * sources
    skipped = jnp.int32(0)
    for begin in piece_starts(here_src, rows, parts, row_devices):
        skipped = skipped + jnp.where(begin + piece <= start, 1, 0).astype(jnp.int32)
    begins = [row * piece // LANES * LANES for row in range(row_devices)]

    @pl.when(skipped == row_devices)
    def _():
        flipped[...] = jnp.zeros_like(flipped)

    for begin in sorted(set(begins)):
        fits = [row for row in range(row_devices) if begins[row] == begin]

        @pl.when((skipped >= fits[0]) & (skipped <= fits[-1]))
        def _(begin=begin):
            if begin:
                flipped[:, :begin] = jnp.zeros((sources, begin), jnp.float32)

            def several(step, carry):
                found = []
                for inner in range(UNROLL):
                    col = step * UNROLL + inner
                    attend = jnp.concatenate(
                        [
                            jnp.concatenate([ref[block, col] for ref in w_refs], axis=0)
                            for block in range(begin // LANES, blocks)
                        ],
                        axis=1,
                    )
                    made = jnp.concatenate(
                        [
                            jnp.concatenate(
                                [
                                    stage[
                                        tile, pl.ds(begin_at + col, span_heads, stride=pitch), :
                                    ].astype(jnp.bfloat16)
                                    for begin_at in slots
                                ],
                                axis=0,
                            )
                            for tile in tiles
                        ],
                        axis=1,
                    )
                    contrib = lax.dot_general(
                        made, attend, (((0,), (0,)), ((), ())), preferred_element_type=jnp.float32
                    )
                    found.append(jnp.sum(jnp.abs(contrib), axis=0, keepdims=True))
                    if len(found) == 8:
                        at = pl.multiple_of(step * UNROLL + inner - 7, 8)
                        flipped[pl.ds(at, 8), begin:] = jnp.concatenate(found, axis=0)
                        found = []
                return carry

            lax.fori_loop(0, sources // UNROLL, several, 0)

    found = flipped[...].T
    o_ref[...] = found if first else before_ref[...] + found


def partial_norms(place, values, projections, weights, before, rows, parts):
    row_devices = len(projections) // parts
    sources = values.shape[0]
    count = weights[0].shape[0] * LANES
    cols = projections[0].shape[-1]
    step = STEP
    kernel = functools.partial(
        norms_kernel,
        rows=rows,
        parts=parts,
        row_devices=row_devices,
        spans=len(weights),
        first=before is None,
    )
    in_specs = [pl.BlockSpec((step, values.shape[1]), lambda b, place: (b, 0))]
    in_specs += [
        pl.BlockSpec(p.shape, lambda b, place: (0, 0), pipeline_mode=pl.Buffered(1))
        for p in projections
    ]
    in_specs += [
        pl.BlockSpec((w.shape[0], step) + w.shape[2:], lambda b, place: (0, b, 0, 0))
        for w in weights
    ]
    args = [values, *projections, *weights]
    out_spec = pl.BlockSpec((count, step), lambda b, place: (0, b))
    if before is not None:
        in_specs.append(out_spec)
        args.append(before)
    return pl.pallas_call(
        kernel,
        out_shape=jax.ShapeDtypeStruct((count, sources), jnp.float32),
        grid_spec=pltpu.PrefetchScalarGridSpec(
            num_scalar_prefetch=1,
            grid=(sources // step,),
            in_specs=in_specs,
            out_specs=out_spec,
            scratch_shapes=[
                pltpu.VMEM((cols // LANES, H * (step + PAD), LANES), jnp.float32),
                pltpu.VMEM((step, count), jnp.float32),
            ],
        ),
        compiler_params=pltpu.CompilerParams(vmem_limit_bytes=60 << 20),
        cost_estimate=pl.CostEstimate(
            flops=count * sources * H * cols + 2 * sources * H * HD * cols,
            transcendentals=0,
            bytes_accessed=count * sources * H * 2,
        ),
        name="partial_norms",
    )(place, *args)


def body(query_rows, key_rows, value_rows, out_proj):
    row_devices = lax.axis_size("row")
    parts = lax.axis_size("src")
    spans = lax.axis_size("width")
    here_row = lax.axis_index("row")
    here_src = lax.axis_index("src")
    here_width = lax.axis_index("width")
    rows, width = query_rows.shape
    col_count, key_width = key_rows.shape
    sources = col_count * parts
    piece = rows // parts

    share = col_count // row_devices
    key_part = lax.dynamic_slice_in_dim(key_rows, here_row * share, share, 0)
    key_part = in_order(gathered(key_part, "src"), "src").reshape(-1, key_width)
    packs = width // key_width
    key_part = key_part.reshape(packs, -1, key_width).transpose(1, 0, 2).reshape(-1, width)
    turn = jnp.where(here_row % 2 == 0, here_src, parts - 1 - here_src)
    mine = lax.dynamic_slice_in_dim(query_rows, turn * piece, piece, 0)
    message = jnp.concatenate([mine, key_part], axis=0)
    messages, origins = line_gather(message, "width")
    place = jnp.stack([here_src, here_row, *origins]).astype(jnp.int32)
    weights = [
        head_weights(place, spread(m, "row"), rows, parts, sources, key_width) for m in messages
    ]
    values = shared_halves(value_rows)

    local_rows, cols = out_proj.shape
    each = cols // row_devices
    chunks = CHUNKS if each % (CHUNKS * LANES) == 0 else 1
    size = each // chunks
    norms = None
    for chunk in range(chunks):
        projections = []
        for bit in range(row_devices):
            at = (here_row ^ bit) * each + chunk * size
            block = lax.dynamic_slice_in_dim(out_proj, at, size, 1)
            if bit:
                block = swapped(block, "row", bit)
            projections += gathered(block, "src")
        norms = partial_norms(place, values, projections, weights, norms, rows, parts)

    stacked = norms.reshape(row_devices, piece, sources)
    held = [
        lax.dynamic_index_in_dim(stacked, here_row ^ bit, 0, keepdims=False)
        for bit in range(row_devices)
    ]
    bit = 1
    while bit < row_devices:
        kept = [held[k] for k in range(0, len(held), 2)]
        sent = [held[k] for k in range(1, len(held), 2)]
        held = [k + swapped(v, "row", bit) for k, v in zip(kept, sent)]
        bit *= 2
    table = held[0]
    total = jnp.pad(jnp.sum(table, axis=1), (0, sources // parts - piece))[None]
    blocks = table.reshape(piece, parts, sources // parts)
    gotten = []
    for shift in range(parts):
        block = lax.dynamic_index_in_dim(blocks, (here_src + shift) % parts, 1, keepdims=False)
        block = jnp.concatenate([block, total], axis=0)
        gotten.append(rotated(block, "src", shift) if shift else block)
    gotten = in_order(gotten, "src")
    gotten = jnp.where(here_row % 2 == 0, gotten, gotten[::-1])
    total = gotten[:, piece, :piece].reshape(rows)
    table = gotten[:, :piece].reshape(rows, -1)
    last = table.shape[1] // spans
    total = total.reshape(-1, last)
    blocks = table.reshape(rows, spans, last)
    summed = None
    for shift in range(spans):
        block = lax.dynamic_index_in_dim(blocks, (here_width + shift) % spans, 1, keepdims=False)
        block = jnp.concatenate([block, total], axis=0)
        block = rotated(block, "width", shift) if shift else block
        summed = block if summed is None else summed + block
    totals = summed[rows:].reshape(rows)
    position = (here_row * rows + jnp.arange(rows, dtype=jnp.int32) + 1).astype(jnp.float32)
    return position[:, None] * summed[:rows] / totals[:, None]


def solution(mesh):
    placed = (P("row", "width"), P("src", "width"), P("src", None), P(("row", "src"), "width"))
    return jax.shard_map(
        body, mesh=mesh, in_specs=placed, out_specs=P("row", ("src", "width")), check_vma=False
    )
```

```python
import functools
import math

import jax
import jax.numpy as jnp
from jax import lax
from jax.experimental import pallas as pl
from jax.experimental.pallas import tpu as pltpu
from jax.sharding import PartitionSpec as P

H = 64
KV = 8
HD = 128
GROUP = H // KV
LANES = 128
FIRST = 256


def rotated(value, axis, shift):
    size = lax.axis_size(axis)
    return lax.ppermute(value, axis, [(k, (k + shift) % size) for k in range(size)])


def gathered(value, axis):
    size = lax.axis_size(axis)
    return [value] + [rotated(value, axis, shift) for shift in range(1, size)]


def in_order(entries, axis):
    size = len(entries)
    here = lax.axis_index(axis)
    stacked = jnp.stack(entries[::-1])
    return jnp.roll(stacked, here + 1, axis=0) if size > 1 else stacked


def swapped(value, axis, bit):
    size = lax.axis_size(axis)
    return lax.ppermute(value, axis, [(k, k ^ bit) for k in range(size)])


def spread(value, count, axis):
    size = lax.axis_size(axis)
    held = {0: value}
    bit = size // 2
    while bit > 1:
        held.update({k | bit: swapped(v[:count], axis, bit) for k, v in list(held.items())})
        bit //= 2
    held.update({k | 1: swapped(v, axis, 1) for k, v in list(held.items())})
    return [held[k] for k in range(size)]


def shared_halves(value):
    count = value.shape[0]
    odd = lax.axis_index("row") % 2
    half = lax.dynamic_slice_in_dim(value, odd * (count // 2), count // 2, 0)
    mine = in_order(gathered(half, "src"), "src")
    other = swapped(mine, "row", 1)
    first = jnp.where(odd == 0, mine, other)
    second = jnp.where(odd == 0, other, mine)
    return jnp.stack([first, second], axis=1).reshape((-1,) + value.shape[1:])


def after(value, earlier):
    return lax.optimization_barrier((value, earlier))[0]


def line_gather(value, axis):
    size = lax.axis_size(axis)
    here = lax.axis_index(axis)
    if size != 4:
        held = [value] + [swapped(value, axis, k) for k in range(1, size)]
        return held, [here ^ k for k in range(size)]
    inner = (here == 1) | (here == 2)
    across, outward = [(1, 2), (2, 1)], [(1, 0), (2, 3)]
    near = swapped(value, axis, 1)
    middle = lax.ppermute(value, axis, across)
    far = lax.ppermute(near, axis, across)
    second = jnp.where(inner, middle, lax.ppermute(middle, axis, outward))
    last = jnp.where(inner, far, lax.ppermute(after(far, second), axis, outward))
    origins = [
        here,
        here ^ 1,
        jnp.array([2, 2, 1, 1], jnp.int32)[here],
        jnp.array([3, 3, 0, 0], jnp.int32)[here],
    ]
    return [value, near, second, last], origins


PAD = 8
UNROLL = 32
HEADS_TOGETHER = 4
STEP = 128


def piece_starts(here_src, rows, parts, row_devices):
    piece = rows // parts
    return [
        row * rows + (here_src if row % 2 == 0 else parts - 1 - here_src) * piece
        for row in range(row_devices)
    ]


def weights_kernel(
    place_ref, *refs, rows, parts, row_devices, sources, limits, scale
):
    pieces = refs[:row_devices]
    o_ref, stage, scales, held, keys = refs[row_devices:]
    here_src, here_row = place_ref[0], place_ref[1]
    piece = rows // parts
    here_heads = held.shape[1] // HD
    key_width = keys.shape[1]
    chunk = math.gcd(rows, 256)
    packs = held.shape[1] // key_width
    pack_rows = pieces[0].shape[0] - piece
    share = sources // parts // 2
    step_at = pl.program_id(0)

    @pl.when(step_at == 0)
    def _():
        for bit, ref in enumerate(pieces[:2]):
            origin = (here_row ^ bit) % 2
            for pack in range(packs):
                src, inner = divmod(pack * pack_rows, share)
                at = src * (sources // parts) + origin * share + inner
                keys[pl.ds(pl.multiple_of(at, pack_rows), pack_rows), :] = ref[
                    piece:, pack * key_width : (pack + 1) * key_width
                ]

    per = max(1, LANES // piece)
    for slot in range(per):
        want = step_at * per + slot
        for bit, ref in enumerate(pieces):

            @pl.when(here_row ^ bit == want)
            def _(ref=ref, slot=slot):
                held[slot * piece : (slot + 1) * piece, :] = ref[:piece, :]

    def folded(value, combine):
        return combine(value.reshape(-1, 8, LANES), axis=0)

    for block, (low, high) in enumerate(limits):

        @pl.when(step_at == block)
        def _(block=block, low=low, high=high):
            local = block * LANES + lax.broadcasted_iota(jnp.int32, (1, LANES), 1)
            row = local // piece
            turn = jnp.where(row % 2 == 0, here_src, parts - 1 - here_src)
            position = row * rows + turn * piece + local % piece
            together = math.gcd(HEADS_TOGETHER, here_heads)

            def several(step, carry):
                for inner in range(together):
                    head = step * together + inner
                    group = head // GROUP
                    query = held[:, pl.ds(pl.multiple_of(head * HD, HD), HD)]
                    columns = pl.ds(pl.multiple_of(group * HD, HD), HD)
                    peak = jnp.full((8, LANES), -1e30, jnp.float32)
                    for at in range(0, high, chunk):
                        scores = lax.dot_general(
                            keys[at : at + chunk, columns],
                            query,
                            (((1,), (1,)), ((), ())),
                            preferred_element_type=jnp.float32,
                        )
                        if at >= low:
                            source = at + lax.broadcasted_iota(jnp.int32, (chunk, LANES), 0)
                            scores = jnp.where(source <= position, scores, jnp.float32(-1e30))
                        stage[head, at : at + chunk, :] = scores
                        peak = jnp.maximum(peak, folded(scores, jnp.max))
                    peak = jnp.max(peak, axis=0, keepdims=True)
                    mass = jnp.zeros((8, LANES), jnp.float32)
                    for at in range(0, high, chunk):
                        grown = jnp.exp2((stage[head, at : at + chunk, :] - peak) * scale)
                        stage[head, at : at + chunk, :] = grown
                        mass = mass + folded(grown, jnp.sum)
                    mass = jnp.sum(mass, axis=0, keepdims=True)
                    scales[pl.ds(pl.multiple_of(head * 8, 8), 8), :] = jnp.broadcast_to(
                        1.0 / mass, (8, LANES)
                    )
                return carry

            lax.fori_loop(0, here_heads // together, several, 0)
            flat = stage.reshape(here_heads * (sources + PAD), LANES)
            factors = scales[pl.ds(0, here_heads, stride=8), :]
            each = 16

            def cast(step, carry):
                for inner in range(each):
                    at = step * each + inner
                    value = flat[pl.ds(at, here_heads, stride=sources + PAD), :]
                    o_ref[at] = (value * factors).astype(jnp.bfloat16)
                return carry

            lax.fori_loop(0, high // each, cast, 0, unroll=2)


def head_weights(place, pieces, rows, parts, sources, key_width):
    width = pieces[0].shape[1]
    row_devices = len(pieces)
    here_heads = width // HD
    piece = rows // parts
    count = piece * row_devices
    blocks = count // LANES
    limits = [
        (
            block * LANES // piece * rows,
            (((block + 1) * LANES - 1) // piece + 1) * rows,
        )
        for block in range(blocks)
    ]
    kernel = functools.partial(
        weights_kernel,
        rows=rows,
        parts=parts,
        row_devices=row_devices,
        sources=sources,
        limits=limits,
        scale=math.log2(math.e) / math.sqrt(HD),
    )
    work = count * sources * here_heads
    return pl.pallas_call(
        kernel,
        out_shape=jax.ShapeDtypeStruct((blocks, sources, here_heads, LANES), jnp.bfloat16),
        grid_spec=pltpu.PrefetchScalarGridSpec(
            num_scalar_prefetch=1,
            grid=(blocks,),
            in_specs=[
                pl.BlockSpec(p.shape, lambda b, place: (0, 0), pipeline_mode=pl.Buffered(1))
                for p in pieces
            ],
            out_specs=pl.BlockSpec(
                (None, sources, here_heads, LANES), lambda b, place: (b, 0, 0, 0)
            ),
            scratch_shapes=[
                pltpu.VMEM((here_heads, sources + PAD, LANES), jnp.float32),
                pltpu.VMEM((here_heads * 8, LANES), jnp.float32),
                pltpu.VMEM((LANES, width), jnp.bfloat16),
                pltpu.VMEM((sources, key_width), jnp.bfloat16),
            ],
        ),
        compiler_params=pltpu.CompilerParams(vmem_limit_bytes=60 << 20),
        cost_estimate=pl.CostEstimate(
            flops=work * HD, transcendentals=work // 2, bytes_accessed=work * 2
        ),
        name="head_weights",
    )(place, *pieces)


def norms_kernel(place_ref, v_ref, *refs, rows, parts, row_devices, spans, first):
    here_src, here_row = place_ref[0], place_ref[1]
    wo_refs = refs[: parts * row_devices]
    w_refs = refs[parts * row_devices : parts * row_devices + spans]
    rest = refs[parts * row_devices + spans :]
    if first:
        o_ref, stage, flipped = rest
    else:
        before_ref, o_ref, stage, flipped = rest
    sources = v_ref.shape[0]
    local_rows, cols = wo_refs[0].shape
    span_heads = H // spans
    local_heads = local_rows // HD
    piece = rows // parts
    pitch = sources + PAD
    tiles = range(cols // LANES)
    blocks = w_refs[0].shape[0]
    for turn in range(parts):
        origin = lax.rem(here_src + parts - turn, parts)
        for bit in range(row_devices):
            base = ((here_row ^ bit) * parts + origin) * local_heads
            for step in range(local_heads):
                head = base + step
                group = head // GROUP
                values = v_ref[:, pl.ds(pl.multiple_of(group * HD, HD), HD)]
                part = wo_refs[bit * parts + turn][step * HD : (step + 1) * HD, :]
                made = jnp.dot(values, part, preferred_element_type=jnp.float32)
                at = pl.multiple_of(head * pitch, PAD)
                for tile in tiles:
                    stage[tile, pl.ds(at, sources), :] = made[:, tile * LANES : (tile + 1) * LANES]

    slots = [place_ref[2 + k] * (span_heads * pitch) for k in range(spans)]
    start = pl.program_id(0) * sources
    skipped = jnp.int32(0)
    for begin in piece_starts(here_src, rows, parts, row_devices):
        skipped = skipped + jnp.where(begin + piece <= start, 1, 0).astype(jnp.int32)
    begins = [row * piece // LANES * LANES for row in range(row_devices)]

    @pl.when(skipped == row_devices)
    def _():
        flipped[...] = jnp.zeros_like(flipped)

    for begin in sorted(set(begins)):
        fits = [row for row in range(row_devices) if begins[row] == begin]

        @pl.when((skipped >= fits[0]) & (skipped <= fits[-1]))
        def _(begin=begin):
            if begin:
                flipped[:, :begin] = jnp.zeros((sources, begin), jnp.float32)

            def several(step, carry):
                found = []
                for inner in range(UNROLL):
                    col = step * UNROLL + inner
                    attend = jnp.concatenate(
                        [
                            jnp.concatenate([ref[block, col] for ref in w_refs], axis=0)
                            for block in range(begin // LANES, blocks)
                        ],
                        axis=1,
                    )
                    made = jnp.concatenate(
                        [
                            jnp.concatenate(
                                [
                                    stage[
                                        tile, pl.ds(begin_at + col, span_heads, stride=pitch), :
                                    ].astype(jnp.bfloat16)
                                    for begin_at in slots
                                ],
                                axis=0,
                            )
                            for tile in tiles
                        ],
                        axis=1,
                    )
                    contrib = lax.dot_general(
                        made, attend, (((0,), (0,)), ((), ())), preferred_element_type=jnp.float32
                    )
                    found.append(jnp.sum(jnp.abs(contrib), axis=0, keepdims=True))
                    if len(found) == 8:
                        at = pl.multiple_of(step * UNROLL + inner - 7, 8)
                        flipped[pl.ds(at, 8), begin:] = jnp.concatenate(found, axis=0)
                        found = []
                return carry

            lax.fori_loop(0, sources // UNROLL, several, 0)

    found = flipped[...].T
    o_ref[...] = found if first else before_ref[...] + found


def partial_norms(place, values, projections, weights, before, rows, parts):
    row_devices = len(projections) // parts
    sources = values.shape[0]
    count = weights[0].shape[0] * LANES
    cols = projections[0].shape[-1]
    step = STEP
    kernel = functools.partial(
        norms_kernel,
        rows=rows,
        parts=parts,
        row_devices=row_devices,
        spans=len(weights),
        first=before is None,
    )
    in_specs = [pl.BlockSpec((step, values.shape[1]), lambda b, place: (b, 0))]
    in_specs += [
        pl.BlockSpec(p.shape, lambda b, place: (0, 0), pipeline_mode=pl.Buffered(1))
        for p in projections
    ]
    in_specs += [
        pl.BlockSpec((w.shape[0], step) + w.shape[2:], lambda b, place: (0, b, 0, 0))
        for w in weights
    ]
    args = [values, *projections, *weights]
    out_spec = pl.BlockSpec((count, step), lambda b, place: (0, b))
    if before is not None:
        in_specs.append(out_spec)
        args.append(before)
    return pl.pallas_call(
        kernel,
        out_shape=jax.ShapeDtypeStruct((count, sources), jnp.float32),
        grid_spec=pltpu.PrefetchScalarGridSpec(
            num_scalar_prefetch=1,
            grid=(sources // step,),
            in_specs=in_specs,
            out_specs=out_spec,
            scratch_shapes=[
                pltpu.VMEM((cols // LANES, H * (step + PAD), LANES), jnp.float32),
                pltpu.VMEM((step, count), jnp.float32),
            ],
        ),
        compiler_params=pltpu.CompilerParams(vmem_limit_bytes=60 << 20),
        cost_estimate=pl.CostEstimate(
            flops=count * sources * H * cols + 2 * sources * H * HD * cols,
            transcendentals=0,
            bytes_accessed=count * sources * H * 2,
        ),
        name="partial_norms",
    )(place, *args)


def whole(query_rows, key_rows, value_rows, out_proj):
    row_devices = lax.axis_size("row")
    parts = lax.axis_size("src")
    spans = lax.axis_size("width")
    here_row = lax.axis_index("row")
    here_src = lax.axis_index("src")
    here_width = lax.axis_index("width")
    rows, width = query_rows.shape
    col_count, key_width = key_rows.shape
    sources = col_count * parts
    piece = rows // parts

    share = col_count // 2
    key_part = lax.dynamic_slice_in_dim(key_rows, here_row % 2 * share, share, 0)
    key_part = in_order(gathered(key_part, "src"), "src").reshape(-1, key_width)
    packs = width // key_width
    key_part = key_part.reshape(packs, -1, key_width).transpose(1, 0, 2).reshape(-1, width)
    turn = jnp.where(here_row % 2 == 0, here_src, parts - 1 - here_src)
    mine = lax.dynamic_slice_in_dim(query_rows, turn * piece, piece, 0)
    message = jnp.concatenate([mine, key_part], axis=0)
    messages, origins = line_gather(message, "width")
    place = jnp.stack([here_src, here_row, *origins]).astype(jnp.int32)
    weights = []
    for m in messages:
        pieces = spread(m, piece, "row")
        weights.append(head_weights(place, pieces, rows, parts, sources, key_width))
    values = shared_halves(value_rows)

    _, cols = out_proj.shape
    each = cols // row_devices
    sizes = [FIRST, each - FIRST] if each > FIRST and each % LANES == 0 else [each]
    norms = None
    begin = 0
    for size in sizes:
        projections = []
        for bit in range(row_devices):
            at = (here_row ^ bit) * each + begin
            block = lax.dynamic_slice_in_dim(out_proj, at, size, 1)
            if bit:
                block = swapped(block, "row", bit)
            projections += gathered(block, "src")
        norms = partial_norms(place, values, projections, weights, norms, rows, parts)
        begin += size

    stacked = norms.reshape(row_devices, piece, sources)
    held = [
        lax.dynamic_index_in_dim(stacked, here_row ^ bit, 0, keepdims=False)
        for bit in range(row_devices)
    ]
    bit = 1
    while bit < row_devices:
        kept = [held[k] for k in range(0, len(held), 2)]
        sent = [held[k] for k in range(1, len(held), 2)]
        held = [k + swapped(v, "row", bit) for k, v in zip(kept, sent)]
        bit *= 2
    table = held[0]
    total = jnp.pad(jnp.sum(table, axis=1), (0, sources // parts - piece))[None]
    blocks = table.reshape(piece, parts, sources // parts)
    gotten = []
    for shift in range(parts):
        block = lax.dynamic_index_in_dim(blocks, (here_src + shift) % parts, 1, keepdims=False)
        block = jnp.concatenate([block, total], axis=0)
        gotten.append(rotated(block, "src", shift) if shift else block)
    gotten = in_order(gotten, "src")
    gotten = jnp.where(here_row % 2 == 0, gotten, gotten[::-1])
    total = gotten[:, piece, :piece].reshape(rows)
    table = gotten[:, :piece].reshape(rows, -1)
    last = table.shape[1] // spans
    total = total.reshape(-1, last)
    blocks = table.reshape(rows, spans, last)
    summed = None
    for shift in range(spans):
        block = lax.dynamic_index_in_dim(blocks, (here_width + shift) % spans, 1, keepdims=False)
        block = jnp.concatenate([block, total], axis=0)
        block = rotated(block, "width", shift) if shift else block
        summed = block if summed is None else summed + block
    totals = summed[rows:].reshape(rows)
    position = (here_row * rows + jnp.arange(rows, dtype=jnp.int32) + 1).astype(jnp.float32)
    return position[:, None] * summed[:rows] / totals[:, None]


def solution(mesh):
    placed = (P("row", "width"), P("src", "width"), P("src", None), P(("row", "src"), "width"))
    return jax.shard_map(
        whole, mesh=mesh, in_specs=placed, out_specs=P("row", ("src", "width")), check_vma=False
    )
```

```python
import functools
import math

import jax
import jax.numpy as jnp
from jax import lax
from jax.experimental import pallas as pl
from jax.experimental.pallas import tpu as pltpu
from jax.sharding import PartitionSpec as P

H = 64
KV = 8
HD = 128
GROUP = H // KV
LANES = 128


def rotated(value, axis, shift):
    size = lax.axis_size(axis)
    return lax.ppermute(value, axis, [(k, (k + shift) % size) for k in range(size)])


def gathered(value, axis):
    size = lax.axis_size(axis)
    return [value] + [rotated(value, axis, shift) for shift in range(1, size)]


def in_order(entries, axis):
    size = len(entries)
    here = lax.axis_index(axis)
    stacked = jnp.stack(entries[::-1])
    return jnp.roll(stacked, here + 1, axis=0) if size > 1 else stacked


def swapped(value, axis, bit):
    size = lax.axis_size(axis)
    return lax.ppermute(value, axis, [(k, k ^ bit) for k in range(size)])


def spread(value, count, axis):
    size = lax.axis_size(axis)
    held = {0: value}
    bit = size // 2
    while bit > 1:
        held.update({k | bit: swapped(v[:count], axis, bit) for k, v in list(held.items())})
        bit //= 2
    held.update({k | 1: swapped(v, axis, 1) for k, v in list(held.items())})
    return [held[k] for k in range(size)]


def shared_halves(value):
    count = value.shape[0]
    odd = lax.axis_index("row") % 2
    half = lax.dynamic_slice_in_dim(value, odd * (count // 2), count // 2, 0)
    mine = in_order(gathered(half, "src"), "src")
    other = swapped(mine, "row", 1)
    first = jnp.where(odd == 0, mine, other)
    second = jnp.where(odd == 0, other, mine)
    return jnp.stack([first, second], axis=1).reshape((-1,) + value.shape[1:])


def after(value, earlier):
    return lax.optimization_barrier((value, earlier))[0]


def line_gather(value, axis):
    size = lax.axis_size(axis)
    here = lax.axis_index(axis)
    if size != 4:
        held = [value] + [swapped(value, axis, k) for k in range(1, size)]
        return held, [here ^ k for k in range(size)]
    inner = (here == 1) | (here == 2)
    across, outward = [(1, 2), (2, 1)], [(1, 0), (2, 3)]
    near = swapped(value, axis, 1)
    middle = lax.ppermute(value, axis, across)
    far = lax.ppermute(near, axis, across)
    second = jnp.where(inner, middle, lax.ppermute(middle, axis, outward))
    last = jnp.where(inner, far, lax.ppermute(after(far, second), axis, outward))
    origins = [
        here,
        here ^ 1,
        jnp.array([2, 2, 1, 1], jnp.int32)[here],
        jnp.array([3, 3, 0, 0], jnp.int32)[here],
    ]
    return [value, near, second, last], origins


PAD = 8
UNROLL = 32
HEADS_TOGETHER = 8
STEP = 128


def piece_starts(here_src, rows, parts, row_devices):
    piece = rows // parts
    return [
        row * rows + (here_src if row % 2 == 0 else parts - 1 - here_src) * piece
        for row in range(row_devices)
    ]


def weights_kernel(
    place_ref, *refs, rows, parts, row_devices, sources, limits, scale
):
    pieces = refs[:row_devices]
    o_ref, stage, scales, held, keys = refs[row_devices:]
    here_src, here_row = place_ref[0], place_ref[1]
    piece = rows // parts
    here_heads = held.shape[1] // HD
    key_width = keys.shape[1]
    chunk = math.gcd(rows, 256)
    packs = held.shape[1] // key_width
    pack_rows = pieces[0].shape[0] - piece
    share = sources // parts // 2
    step_at = pl.num_programs(0) - 1 - pl.program_id(0)
    half_at = pl.program_id(1)
    half = sources // 2

    @pl.when((pl.program_id(0) == 0) & (half_at == 0))
    def _():
        for bit, ref in enumerate(pieces[:2]):
            origin = (here_row ^ bit) % 2
            for pack in range(packs):
                src, inner = divmod(pack * pack_rows, share)
                at = src * (sources // parts) + origin * share + inner
                keys[pl.ds(pl.multiple_of(at, pack_rows), pack_rows), :] = ref[
                    piece:, pack * key_width : (pack + 1) * key_width
                ]

    per = max(1, LANES // piece)
    for slot in range(per):
        want = step_at * per + slot
        for bit, ref in enumerate(pieces):

            @pl.when((here_row ^ bit == want) & (half_at == 0))
            def _(ref=ref, slot=slot):
                held[slot * piece : (slot + 1) * piece, :] = ref[:piece, :]

    def folded(value, combine):
        return combine(value.reshape(-1, 8, LANES), axis=0)

    for block, (low, high) in enumerate(limits):

        @pl.when((step_at == block) & (half_at == 0))
        def _(block=block, low=low, high=high):
            local = block * LANES + lax.broadcasted_iota(jnp.int32, (1, LANES), 1)
            row = local // piece
            turn = jnp.where(row % 2 == 0, here_src, parts - 1 - here_src)
            position = row * rows + turn * piece + local % piece
            together = math.gcd(HEADS_TOGETHER, here_heads)

            def several(step, carry):
                for inner in range(together):
                    head = step * together + inner
                    group = head // GROUP
                    query = held[:, pl.ds(pl.multiple_of(head * HD, HD), HD)]
                    columns = pl.ds(pl.multiple_of(group * HD, HD), HD)
                    peak = jnp.full((8, LANES), -1e30, jnp.float32)
                    for at in range(0, high, chunk):
                        scores = lax.dot_general(
                            keys[at : at + chunk, columns],
                            query,
                            (((1,), (1,)), ((), ())),
                            preferred_element_type=jnp.float32,
                        )
                        if at >= low:
                            source = at + lax.broadcasted_iota(jnp.int32, (chunk, LANES), 0)
                            scores = jnp.where(source <= position, scores, jnp.float32(-1e30))
                        stage[head, at : at + chunk, :] = scores
                        peak = jnp.maximum(peak, folded(scores, jnp.max))
                    peak = jnp.max(peak, axis=0, keepdims=True)
                    mass = jnp.zeros((8, LANES), jnp.float32)
                    for at in range(0, high, chunk):
                        grown = jnp.exp2((stage[head, at : at + chunk, :] - peak) * scale)
                        stage[head, at : at + chunk, :] = grown
                        mass = mass + folded(grown, jnp.sum)
                    mass = jnp.sum(mass, axis=0, keepdims=True)
                    scales[pl.ds(pl.multiple_of(head * 8, 8), 8), :] = jnp.broadcast_to(
                        1.0 / mass, (8, LANES)
                    )
                return carry

            lax.fori_loop(0, here_heads // together, several, 0)

    flat = stage.reshape(here_heads * (sources + PAD), LANES)
    factors = scales[pl.ds(0, here_heads, stride=8), :]
    each = 16
    top = (((step_at + 1) * LANES - 1) // piece + 1) * rows
    count = jnp.clip(top - half_at * half, 0, half)

    def cast(step, carry):
        for inner in range(each):
            at = step * each + inner
            value = flat[pl.ds(half_at * half + at, here_heads, stride=sources + PAD), :]
            o_ref[at] = (value * factors).astype(jnp.bfloat16)
        return carry

    lax.fori_loop(0, count // each, cast, 0)


def head_weights(place, pieces, rows, parts, sources, key_width):
    width = pieces[0].shape[1]
    row_devices = len(pieces)
    here_heads = width // HD
    piece = rows // parts
    count = piece * row_devices
    blocks = count // LANES
    limits = [
        (
            block * LANES // piece * rows,
            (((block + 1) * LANES - 1) // piece + 1) * rows,
        )
        for block in range(blocks)
    ]
    kernel = functools.partial(
        weights_kernel,
        rows=rows,
        parts=parts,
        row_devices=row_devices,
        sources=sources,
        limits=limits,
        scale=math.log2(math.e) / math.sqrt(HD),
    )
    work = count * sources * here_heads

    def written(b, j, place):
        block = blocks - 1 - b
        top = (((block + 1) * LANES - 1) // piece + 1) * rows
        return block, jnp.where(top > sources // 2, j, 0), 0, 0

    return pl.pallas_call(
        kernel,
        out_shape=jax.ShapeDtypeStruct((blocks, sources, here_heads, LANES), jnp.bfloat16),
        grid_spec=pltpu.PrefetchScalarGridSpec(
            num_scalar_prefetch=1,
            grid=(blocks, 2),
            in_specs=[
                pl.BlockSpec(p.shape, lambda b, j, place: (0, 0), pipeline_mode=pl.Buffered(1))
                for p in pieces
            ],
            out_specs=pl.BlockSpec((None, sources // 2, here_heads, LANES), written),
            scratch_shapes=[
                pltpu.VMEM((here_heads, sources + PAD, LANES), jnp.float32),
                pltpu.VMEM((here_heads * 8, LANES), jnp.float32),
                pltpu.VMEM((LANES, width), jnp.bfloat16),
                pltpu.VMEM((sources, key_width), jnp.bfloat16),
            ],
        ),
        compiler_params=pltpu.CompilerParams(vmem_limit_bytes=60 << 20),
        cost_estimate=pl.CostEstimate(
            flops=work * HD, transcendentals=work // 2, bytes_accessed=work * 2
        ),
        name="head_weights",
    )(place, *pieces)


def norms_kernel(place_ref, v_ref, *refs, rows, parts, row_devices, spans):
    here_src, here_row = place_ref[0], place_ref[1]
    wo_refs = refs[: parts * row_devices]
    w_refs = refs[parts * row_devices : parts * row_devices + spans]
    o_ref, stage, flipped = refs[parts * row_devices + spans :]
    sources = v_ref.shape[0]
    local_rows, cols = wo_refs[0].shape
    span_heads = H // spans
    local_heads = local_rows // HD
    piece = rows // parts
    pitch = sources + PAD
    tiles = range(cols // LANES)
    blocks = w_refs[0].shape[0]
    for turn in range(parts):
        origin = lax.rem(here_src + parts - turn, parts)
        for bit in range(row_devices):
            base = ((here_row ^ bit) * parts + origin) * local_heads
            for step in range(local_heads):
                head = base + step
                group = head // GROUP
                values = v_ref[:, pl.ds(pl.multiple_of(group * HD, HD), HD)]
                part = wo_refs[bit * parts + turn][step * HD : (step + 1) * HD, :]
                made = jnp.dot(values, part, preferred_element_type=jnp.float32)
                at = pl.multiple_of(head * pitch, PAD)
                for tile in tiles:
                    stage[tile, pl.ds(at, sources), :] = made[:, tile * LANES : (tile + 1) * LANES]

    slots = [place_ref[2 + k] * (span_heads * pitch) for k in range(spans)]
    start = pl.program_id(0) * sources
    skipped = jnp.int32(0)
    for begin in piece_starts(here_src, rows, parts, row_devices):
        skipped = skipped + jnp.where(begin + piece <= start, 1, 0).astype(jnp.int32)
    begins = [row * piece // LANES * LANES for row in range(row_devices)]

    @pl.when(skipped == row_devices)
    def _():
        flipped[...] = jnp.zeros_like(flipped)

    for begin in sorted(set(begins)):
        fits = [row for row in range(row_devices) if begins[row] == begin]

        @pl.when((skipped >= fits[0]) & (skipped <= fits[-1]))
        def _(begin=begin):
            if begin:
                flipped[:, :begin] = jnp.zeros((sources, begin), jnp.float32)
            unroll = UNROLL if begin else UNROLL // 2

            def several(step, carry):
                found = []
                for inner in range(unroll):
                    col = step * unroll + inner
                    attend = jnp.concatenate(
                        [
                            jnp.concatenate([ref[block, col] for ref in w_refs], axis=0)
                            for block in range(begin // LANES, blocks)
                        ],
                        axis=1,
                    )
                    made = jnp.concatenate(
                        [
                            jnp.concatenate(
                                [
                                    stage[
                                        tile, pl.ds(begin_at + col, span_heads, stride=pitch), :
                                    ].astype(jnp.bfloat16)
                                    for begin_at in slots
                                ],
                                axis=0,
                            )
                            for tile in tiles
                        ],
                        axis=1,
                    )
                    contrib = lax.dot_general(
                        made, attend, (((0,), (0,)), ((), ())), preferred_element_type=jnp.float32
                    )
                    found.append(jnp.sum(jnp.abs(contrib), axis=0, keepdims=True))
                    if len(found) == 8:
                        at = pl.multiple_of(step * unroll + inner - 7, 8)
                        flipped[pl.ds(at, 8), begin:] = jnp.concatenate(found, axis=0)
                        found = []
                return carry

            lax.fori_loop(0, sources // unroll, several, 0)

    o_ref[...] = flipped[...].T


def partial_norms(place, values, projections, weights, rows, parts):
    row_devices = len(projections) // parts
    sources = values.shape[0]
    count = weights[0].shape[0] * LANES
    cols = projections[0].shape[-1]
    step = STEP
    kernel = functools.partial(
        norms_kernel,
        rows=rows,
        parts=parts,
        row_devices=row_devices,
        spans=len(weights),
    )
    in_specs = [pl.BlockSpec((step, values.shape[1]), lambda b, place: (b, 0))]
    in_specs += [
        pl.BlockSpec(p.shape, lambda b, place: (0, 0), pipeline_mode=pl.Buffered(1))
        for p in projections
    ]
    in_specs += [
        pl.BlockSpec((w.shape[0], step) + w.shape[2:], lambda b, place: (0, b, 0, 0))
        for w in weights
    ]
    args = [values, *projections, *weights]
    out_spec = pl.BlockSpec((count, step), lambda b, place: (0, b))
    return pl.pallas_call(
        kernel,
        out_shape=jax.ShapeDtypeStruct((count, sources), jnp.float32),
        grid_spec=pltpu.PrefetchScalarGridSpec(
            num_scalar_prefetch=1,
            grid=(sources // step,),
            in_specs=in_specs,
            out_specs=out_spec,
            scratch_shapes=[
                pltpu.VMEM((cols // LANES, H * (step + PAD), LANES), jnp.float32),
                pltpu.VMEM((step, count), jnp.float32),
            ],
        ),
        compiler_params=pltpu.CompilerParams(vmem_limit_bytes=60 << 20),
        cost_estimate=pl.CostEstimate(
            flops=count * sources * H * cols + 2 * sources * H * HD * cols,
            transcendentals=0,
            bytes_accessed=count * sources * H * 2,
        ),
        name="partial_norms",
    )(place, *args)


def whole(query_rows, key_rows, value_rows, out_proj):
    row_devices = lax.axis_size("row")
    parts = lax.axis_size("src")
    spans = lax.axis_size("width")
    here_row = lax.axis_index("row")
    here_src = lax.axis_index("src")
    here_width = lax.axis_index("width")
    rows, width = query_rows.shape
    col_count, key_width = key_rows.shape
    sources = col_count * parts
    piece = rows // parts

    share = col_count // 2
    key_part = lax.dynamic_slice_in_dim(key_rows, here_row % 2 * share, share, 0)
    key_part = in_order(gathered(key_part, "src"), "src").reshape(-1, key_width)
    packs = width // key_width
    key_part = key_part.reshape(packs, -1, key_width).transpose(1, 0, 2).reshape(-1, width)
    turn = jnp.where(here_row % 2 == 0, here_src, parts - 1 - here_src)
    mine = lax.dynamic_slice_in_dim(query_rows, turn * piece, piece, 0)
    message = jnp.concatenate([mine, key_part], axis=0)
    messages, origins = line_gather(message, "width")
    place = jnp.stack([here_src, here_row, *origins]).astype(jnp.int32)
    weights = []
    for m in messages:
        pieces = spread(m, piece, "row")
        weights.append(head_weights(place, pieces, rows, parts, sources, key_width))
    values = shared_halves(value_rows)

    _, cols = out_proj.shape
    each = cols // row_devices
    projections = []
    for bit in range(row_devices):
        block = lax.dynamic_slice_in_dim(out_proj, (here_row ^ bit) * each, each, 1)
        if bit:
            block = swapped(block, "row", bit)
        projections += gathered(block, "src")
    norms = partial_norms(place, values, projections, weights, rows, parts)

    stacked = norms.reshape(row_devices, piece, sources)
    held = [
        lax.dynamic_index_in_dim(stacked, here_row ^ bit, 0, keepdims=False)
        for bit in range(row_devices)
    ]
    bit = 1
    while bit < row_devices:
        kept = [held[k] for k in range(0, len(held), 2)]
        sent = [held[k] for k in range(1, len(held), 2)]
        held = [k + swapped(v, "row", bit) for k, v in zip(kept, sent)]
        bit *= 2
    table = held[0]
    total = jnp.pad(jnp.sum(table, axis=1), (0, sources // parts - piece))[None]
    blocks = table.reshape(piece, parts, sources // parts)
    gotten = []
    for shift in range(parts):
        block = lax.dynamic_index_in_dim(blocks, (here_src + shift) % parts, 1, keepdims=False)
        block = jnp.concatenate([block, total], axis=0)
        gotten.append(rotated(block, "src", shift) if shift else block)
    gotten = in_order(gotten, "src")
    gotten = jnp.where(here_row % 2 == 0, gotten, gotten[::-1])
    total = gotten[:, piece, :piece].reshape(rows)
    table = gotten[:, :piece].reshape(rows, -1)
    last = table.shape[1] // spans
    total = total.reshape(-1, last)
    blocks = table.reshape(rows, spans, last)
    summed = None
    for shift in range(spans):
        block = lax.dynamic_index_in_dim(blocks, (here_width + shift) % spans, 1, keepdims=False)
        block = jnp.concatenate([block, total], axis=0)
        block = rotated(block, "width", shift) if shift else block
        summed = block if summed is None else summed + block
    totals = summed[rows:].reshape(rows)
    position = (here_row * rows + jnp.arange(rows, dtype=jnp.int32) + 1).astype(jnp.float32)
    return position[:, None] * summed[:rows] / totals[:, None]


def solution(mesh):
    placed = (P("row", "width"), P("src", "width"), P("src", None), P(("row", "src"), "width"))
    return jax.shard_map(
        whole, mesh=mesh, in_specs=placed, out_specs=P("row", ("src", "width")), check_vma=False
    )
```
